32 devices in a mesh: row: 8 (over z, x), col: 4 (over y, core).
Axes of the slice: x: 2, y: 2, z: 4, core: 2. Of those that a mesh axis runs over, the one named last changes fastest.
Arguments:
- inverse: float32 [12288, 12288], P('row', 'col'), may hold values from -0.21875 to 0.21875
- pattern: int32 [24, 24], replicated, may hold values from 0 to 1, as said below
- factor: float32 [12288, 1024], P(('row', 'col')), may hold values from -0.4375 to 0.4375
- diag_inverse: float32 [1024, 1024], replicated, may hold values from -6 to 6
Outputs:
- panel_out: float32 [12288, 1024], P(('row', 'col'))
- diag_block: float32 [1024, 1024], replicated
The draws below stay inside these ranges and needn't reach their ends.
Inputs may be any that keep to these rules, and one draw needn't show every extreme that they name: pattern[i, j] is 1 where tile (i, j) of the inverse is stored, else 0.
All inputs are finite; a program needn't handle non-finite values.
Results may differ from the reference program's by a relative error of at most 0.000075.
Values sent between devices are 32-bit elements; how exact they have to be, the bound alone decides.
No kernel may reach another device: no remote copies, remote signals or barrier semaphores. Data moves between devices by JAX's collectives and lax.ppermute only.
A program may use at most 128 MiB of HBM per device.

```python
import jax
import jax.numpy as jnp
from jax import lax

B = 512
W = 1024
TILES = 24
ANC = 12288
N_ROW = 8
N_COL = 4


def draw_pattern(key, part):
    level_key = jax.random.fold_in(key, 11)
    roll_key = jax.random.fold_in(key, 12)
    exponent = jax.random.randint(level_key, (N_ROW, N_COL), 0, 4)
    levels = jnp.power(2, exponent).astype(jnp.int32)
    spread_levels = jnp.repeat(jnp.repeat(levels, TILES // N_ROW, 0), TILES // N_COL, 1)
    rolls = jax.random.randint(roll_key, (TILES, TILES), 0, 8)
    return (rolls < spread_levels).astype(jnp.int32)


def block_levels(key, shape, cuts, low, high):
    level = 1.0
    for position, parts in cuts:
        draws = jax.random.uniform(jax.random.fold_in(jax.random.fold_in(key, 6), position), (parts,), jnp.float32, low / len(cuts), high / len(cuts))
        level = level * jnp.repeat(jnp.exp(draws), shape[position] // parts).reshape((-1,) + (1,) * (len(shape) - 1 - position))
    return level


def bell_draw(stream_key, dims, width, most, split=(), kind=jnp.bfloat16):
    values = width * jax.random.normal(stream_key, dims, jnp.float32)
    if split:
        values = values * block_levels(stream_key, dims, split, -0.22, 0.18)
    return jnp.clip(values, -most, most).astype(kind)


def setup_inputs(seed: int = 0) -> dict:
    splits = jax.random.split(jax.random.key(seed), 5)
    inverse = bell_draw(splits[0], (ANC, ANC), (ANC // 16) ** -0.5, 0.21875, ((0, 8), (1, 4)), jnp.float32)
    pattern = draw_pattern(jax.random.fold_in(splits[4], 71), 0)
    factor = bell_draw(splits[2], (ANC, W), (ANC // 64) ** -0.5, 0.4375, ((0, 32),), jnp.float32)
    diag_inverse = bell_draw(splits[3], (W, W), 1.0, 6.0, (), jnp.float32)
    return {"inverse": inverse, "pattern": pattern, "factor": factor, "diag_inverse": diag_inverse}


HIGHEST = lax.Precision.HIGHEST


def reference(inverse, pattern, factor, diag_inverse):
    def strip_product(tile_index):
        row_strip = lax.dynamic_slice_in_dim(inverse, tile_index * B, B, 0)
        keep_mask = jnp.repeat(pattern[tile_index], B).astype(row_strip.dtype)
        return jnp.dot(row_strip * keep_mask[None, :], factor, precision=HIGHEST)

    products = lax.map(strip_product, jnp.arange(TILES, dtype=jnp.int32))
    panel_out = -products.reshape(ANC, W)
    diag_block = diag_inverse - jnp.dot(factor.T, panel_out, precision=HIGHEST)
    return panel_out, diag_block
```

```python
import functools

import jax
import jax.numpy as jnp
from jax import lax
from jax.experimental import pallas as pl
from jax.experimental.pallas import tpu as pltpu
from jax.sharding import Mesh, PartitionSpec as P


B = 512
LANES = 128
SHARES = (1, 2, 2, 2, 1)
GROUPS = ((0,), (1, 2), (3, 4))
AHEAD = 2
OFFLOADED = (0,)
DEPTH = 4

CHIPS = ("z", "x", "y")
COLUMN = ("y", "k")
DEVICES = ("z", "x", "y", "k")
VMEM = pl.BlockSpec(memory_space=pltpu.VMEM)
SMEM = pl.BlockSpec(memory_space=pltpu.SMEM)
ANY = pl.BlockSpec(memory_space=pl.ANY)


def split(value):
    high = value.astype(jnp.bfloat16)
    low = (value - high.astype(jnp.float32)).astype(jnp.bfloat16)
    return high, low


def dot(left, right):
    return jnp.dot(left, right, preferred_element_type=jnp.float32)


def halve_kernel(tile_cols, tiles_ref, count_ref, inverse_ref, out_ref, held, made, sems, out_sems):
    count = count_ref[0]

    def fetch(step, slot):
        chosen = tiles_ref[step]
        row = pl.multiple_of(chosen // tile_cols * B, B)
        col = pl.multiple_of(chosen % tile_cols * B, B)
        return pltpu.make_async_copy(
            inverse_ref.at[pl.ds(row, B), pl.ds(col, B)], held.at[slot], sems.at[slot]
        )

    def put(step, slot):
        return pltpu.make_async_copy(made.at[slot], out_ref.at[step], out_sems.at[slot])

    for ahead in range(DEPTH - 1):

        @pl.when(ahead < count)
        def _():
            fetch(ahead, ahead).start()

    def step(index, carry):
        slot = lax.rem(index, DEPTH)
        side = lax.rem(index, 2)

        @pl.when(index + DEPTH - 1 < count)
        def _():
            fetch(index + DEPTH - 1, lax.rem(index + DEPTH - 1, DEPTH)).start()

        fetch(index, slot).wait()

        @pl.when(index >= 2)
        def _():
            put(index - 2, side).wait()

        high, low = split(held[slot])
        made[side, :, :B] = high
        made[side, :, B:] = low
        put(index, side).start()
        return carry

    lax.fori_loop(0, count, step, 0)
    for back in (2, 1):

        @pl.when(count >= back)
        def _():
            put(count - back, lax.rem(count - back, 2)).wait()


def halve(tiles, count, inverse):
    tile_rows, tile_cols = inverse.shape[0] // B, inverse.shape[1] // B
    return pl.pallas_call(
        functools.partial(halve_kernel, tile_cols),
        out_shape=jax.ShapeDtypeStruct((tile_rows * tile_cols, B, 2 * B), jnp.bfloat16),
        in_specs=[SMEM, SMEM, ANY],
        out_specs=ANY,
        scratch_shapes=[
            pltpu.VMEM((DEPTH, B, B), jnp.float32),
            pltpu.VMEM((2, B, 2 * B), jnp.bfloat16),
            pltpu.SemaphoreType.DMA((DEPTH,)),
            pltpu.SemaphoreType.DMA((2,)),
        ],
        cost_estimate=pl.CostEstimate(
            flops=0, bytes_accessed=8 * inverse.size, transcendentals=0
        ),
        name="halve",
    )(tiles, count, inverse)


def tiles_kernel(tile_cols, parts, tiles_ref, count_ref, place_ref, parts_ref, *refs):
    part_refs = refs[:parts]
    keep_ref, send_ref, highs, lows, total, held, came, sems, came_sems, out_sems = refs[parts:]
    count = count_ref[0]
    x, z, k = place_ref[0], place_ref[1], place_ref[2]
    cols, rows_each = part_refs[0].shape[0], part_refs[0].shape[1]

    def fetch(step, slot):
        return pltpu.make_async_copy(parts_ref.at[step], held.at[slot], sems.at[slot])

    for ahead in range(DEPTH - 1):

        @pl.when(ahead < count)
        def _():
            fetch(ahead, ahead).start()

    arrivals = [
        pltpu.make_async_copy(part_ref, came.at[index], came_sems.at[index])
        for index, part_ref in enumerate(part_refs)
    ]
    for arrival in arrivals:
        arrival.start()
    total[...] = jnp.zeros_like(total)
    for index in range(parts):
        half = lax.bitwise_xor(x, index) if parts == 2 else 0
        arrivals[index].wait()
        for j in range(cols):
            origin = lax.rem(z + j, cols)
            first = pl.multiple_of((half * cols + origin) * rows_each, rows_each)
            high, low = split(came[index, j])
            highs[pl.ds(first, rows_each), :] = high
            lows[pl.ds(first, rows_each), :] = low

    def step(index, carry):
        slot = lax.rem(index, DEPTH)

        @pl.when(index + DEPTH - 1 < count)
        def _():
            fetch(index + DEPTH - 1, lax.rem(index + DEPTH - 1, DEPTH)).start()

        fetch(index, slot).wait()
        chosen = tiles_ref[index]
        row = pl.multiple_of(chosen // tile_cols * B, B)
        col = pl.multiple_of(chosen % tile_cols * B, B)
        high, low = highs[pl.ds(col, B), :], lows[pl.ds(col, B), :]
        width = total.shape[1]
        if width == LANES:
            both = dot(held[slot, :, :B], jnp.concatenate([high, low], axis=1))
            product = both[:, :width] + both[:, width:] + dot(held[slot, :, B:], high)
        else:
            product = (
                dot(held[slot, :, :B], high)
                + dot(held[slot, :, B:], high)
                + dot(held[slot, :, :B], low)
            )
        total[pl.ds(row, B), :] += product
        return carry

    lax.fori_loop(0, count, step, 0)
    pairs, rows_out = keep_ref.shape[0], keep_ref.shape[1]
    copies = []
    for index, (out_ref, side) in enumerate(((send_ref, 1 - k), (keep_ref, k))):
        for pair in range(pairs):
            first = pl.multiple_of((2 * pair + side) * rows_out, rows_out)
            copies.append(
                pltpu.make_async_copy(
                    total.at[pl.ds(first, rows_out), :],
                    out_ref.at[pair],
                    out_sems.at[index * pairs + pair],
                )
            )
    for copy in copies:
        copy.start()
    for copy in copies:
        copy.wait()


def tile_products(tiles, count, place, halved, parts, rows, tile_cols):
    cols, _, width = parts[0].shape
    out = jax.ShapeDtypeStruct((cols // 2, rows // cols, width), jnp.float32)
    return pl.pallas_call(
        functools.partial(tiles_kernel, tile_cols, len(parts)),
        out_shape=(out, out),
        in_specs=[SMEM, SMEM, SMEM, ANY] + [ANY] * len(parts),
        out_specs=(ANY, ANY),
        scratch_shapes=[
            pltpu.VMEM((tile_cols * B, width), jnp.bfloat16),
            pltpu.VMEM((tile_cols * B, width), jnp.bfloat16),
            pltpu.VMEM((rows, width), jnp.float32),
            pltpu.VMEM((DEPTH, B, 2 * B), jnp.bfloat16),
            pltpu.VMEM((len(parts), *parts[0].shape), jnp.float32),
            pltpu.SemaphoreType.DMA((DEPTH,)),
            pltpu.SemaphoreType.DMA((len(parts),)),
            pltpu.SemaphoreType.DMA((cols,)),
        ],
        cost_estimate=pl.CostEstimate(
            flops=6 * rows * tile_cols * B * width,
            bytes_accessed=4 * rows * tile_cols * B,
            transcendentals=0,
        ),
        name="tiles",
    )(tiles, count, place, halved, *parts)


def turn_kernel(pairs, place_ref, *refs):
    out_ref = refs[-1]
    for index in range(pairs):
        value = refs[index][...] if pairs == 2 else refs[0][index]
        rows = value.shape[0]
        if pairs == 2:
            side = lax.bitwise_xor(place_ref[3], index)
            where = pl.ds(pl.multiple_of(side * rows, rows), rows)
        else:
            where = slice(index * rows, (index + 1) * rows)
        high, low = split(value.T)
        out_ref[0, :, where] = high
        out_ref[1, :, where] = low


def turn(place, factors, pairs, rows, width):
    return pl.pallas_call(
        functools.partial(turn_kernel, pairs),
        out_shape=jax.ShapeDtypeStruct((2, width, pairs * rows), jnp.bfloat16),
        in_specs=[SMEM] + [VMEM] * len(factors),
        out_specs=VMEM,
        name="turn",
    )(place, *factors)


def finish_kernel(swapped, place_ref, kept_ref, came_ref, turned_ref, sum_ref, term_ref):
    pairs, rows, width = kept_ref.shape
    for pair in range(pairs):
        sum_ref[pair] = kept_ref[pair] + came_ref[pair]
    high, low = split(sum_ref[...].reshape(pairs * rows, width))
    half = term_ref.shape[1]
    for index in range(2):
        side = lax.bitwise_xor(place_ref[2], index) if swapped else index
        left = pl.ds(pl.multiple_of(side * half, half), half)
        term_ref[index] = (
            dot(turned_ref[0, left, :], high)
            + dot(turned_ref[1, left, :], high)
            + dot(turned_ref[0, left, :], low)
        )


def finish(place, kept, came, turned, swapped):
    pairs, rows, step = kept.shape
    width = turned.shape[1]
    return pl.pallas_call(
        functools.partial(finish_kernel, swapped),
        out_shape=(
            jax.ShapeDtypeStruct(kept.shape, jnp.float32),
            jax.ShapeDtypeStruct((2, width // 2, step), jnp.float32),
        ),
        in_specs=[SMEM, VMEM, VMEM, VMEM],
        out_specs=(VMEM, VMEM),
        cost_estimate=pl.CostEstimate(
            flops=6 * pairs * rows * width * step,
            bytes_accessed=4 * pairs * rows * (width + 3 * step) + 4 * width * step,
            transcendentals=0,
        ),
        name="finish",
    )(place, kept, came, turned)


def stored_list(pattern, first_row, first_col, tile_rows, tile_cols):
    window = lax.dynamic_slice(pattern, (first_row, first_col), (tile_rows, tile_cols)).reshape(-1)
    count_all = tile_rows * tile_cols
    order = jnp.cumsum(window) - 1
    slots = jnp.arange(count_all, dtype=jnp.int32)
    chosen = (order[None, :] == slots[:, None]) & (window[None, :] > 0)
    return jnp.sum(jnp.where(chosen, slots[None, :], 0), axis=1), jnp.sum(window)[None]


def swap(value, axis):
    return lax.ppermute(value, axis, [(0, 1), (1, 0)])


def sum_scatter(value, axes):
    return jnp.sum(lax.all_to_all(value, axes, split_axis=0, concat_axis=0), axis=0)


def spread(value, axes):
    copies = jnp.broadcast_to(value[None], (lax.axis_size(axes), *value.shape))
    return lax.all_to_all(copies, axes, split_axis=0, concat_axis=0)


def pick(pair, index):
    return lax.dynamic_index_in_dim(pair, index, 0, False)


def routes(planes, cols, turn_index):
    ratio = 2 * planes // cols
    pairs = []
    for z in range(planes):
        for x in range(2):
            for col in range(cols):
                if ratio == 1 and col % 2 != x:
                    continue
                source = ((col * ratio // 2) * 2 + x) * cols + (z + turn_index) % cols
                pairs.append((source, (z * 2 + x) * cols + col))
    return pairs


def shares(width):
    return SHARES if sum(SHARES) * LANES == width else (1,) * (width // LANES)


def after(value, others):
    return lax.optimization_barrier((value, others))[0]


def step_body(inverse, pattern, factor, diag_inverse):
    planes, cols = lax.axis_size("z"), lax.axis_size(COLUMN)
    x, y, z, k = (lax.axis_index(a) for a in ("x", "y", "z", "k"))
    column = lax.axis_index(COLUMN)
    ratio = 2 * planes // cols
    rows_each, width = factor.shape
    tile_rows, tile_cols = inverse.shape[0] // B, inverse.shape[1] // B
    tiles, count = stored_list(
        pattern, (z * 2 + x) * tile_rows, column * tile_cols, tile_rows, tile_cols
    )
    place = jnp.stack([x, z, k, y]).astype(jnp.int32)
    chips = lax.axis_size(CHIPS)
    pairs = cols // 2
    if pairs == 2:
        factors = (factor, swap(factor, "y"))
    else:
        factors = (lax.all_gather(factor, "y", axis=0),)
    halved = halve(tiles, count, inverse)
    turned = turn(place, factors, pairs, rows_each, width)
    arrivals, panels, terms = [], [], []
    pieces, spreads, pending, diags = {}, {}, {}, {}
    first = 0
    groups = groups_of(len(shares(width)))
    for chunk, share in enumerate(shares(width)):
        step = share * LANES
        part = factor[:, first : first + step]
        first += step
        if chunk >= AHEAD:
            part = after(part, arrivals[chunk - AHEAD])
        mine = []
        for j in range(cols):
            mine.append(lax.ppermute(part, DEVICES, routes(planes, cols, j)))
        arrivals.append(mine)
        mine = jnp.stack(mine)
        theirs = swap(mine, "x")
        parts = (mine, theirs) if ratio == 2 else (jnp.where(column % 2 == x, mine, theirs),)
        gate = after(place, pieces[chunk - 2]) if chunk - 2 in pieces else place
        kept, send = tile_products(tiles, count, gate, halved, parts, inverse.shape[0], tile_cols)
        for index, (born, state, value) in list(pending.items()):
            value = after(value, kept)
            if state == 0:
                piece = jnp.sum(value, axis=0)
                pieces[chunk - 1] = piece
                pending[index] = (born, 1, spread(piece, CHIPS))
            else:
                spreads[born] = value
                del pending[index]
                diags[index] = assemble(value, width, k)
        came = swap(send, "k")
        gate = after(place, spreads[chunk - 2]) if chunk - 2 in spreads else place
        summed, term = finish(gate, kept, came, turned, chunk not in groups[0])
        terms.append(term)
        if pairs == 2:
            panels.append(-(pick(summed, y) + swap(pick(summed, 1 - y), "y")))
        else:
            panels.append(-sum_scatter(summed, "y"))
        for index, group in enumerate(groups):
            if not group or group[-1] != chunk:
                continue
            mine = [terms[member] for member in group]
            if index in OFFLOADED:
                diags[index] = lax.psum([term.reshape(width, -1) for term in mine], DEVICES)
                continue
            half = jnp.concatenate([term[0] for term in mine], 1) + swap(
                jnp.concatenate([term[1] for term in mine], 1), "k"
            )
            sent = half.reshape(chips, -1, half.shape[1])
            value = lax.all_to_all(sent, CHIPS, split_axis=0, concat_axis=0)
            pending[index] = (chunk, 0, value)
    for index, (_, state, value) in sorted(pending.items()):
        if state == 0:
            value = spread(jnp.sum(value, axis=0), CHIPS)
        diags[index] = assemble(value, width, k)
    diags = [piece for index in sorted(diags) for piece in diags[index]]
    return jnp.concatenate(panels, 1), diag_inverse + jnp.concatenate(diags, 1)


def assemble(value, width, k):
    full = value.reshape(width // 2, -1)
    far = swap(full, "k")
    return [jnp.concatenate([jnp.where(k == 0, full, far), jnp.where(k == 0, far, full)], 0)]


def groups_of(chunks):
    return GROUPS if chunks == len(SHARES) else ((), tuple(range(chunks)))


def solution(mesh):
    rows, cols = mesh.shape["row"], mesh.shape["col"]
    grid = Mesh(mesh.devices.reshape(rows // 2, 2, cols // 2, 2), DEVICES)
    return jax.shard_map(
        step_body,
        mesh=grid,
        in_specs=(P(("z", "x"), ("y", "k")), P(), P(DEVICES, None), P()),
        out_specs=(P(DEVICES, None), P()),
        check_vma=False,
    )
```

```python
import functools

import jax
import jax.numpy as jnp
from jax import lax
from jax.experimental import pallas as pl
from jax.experimental.pallas import tpu as pltpu
from jax.sharding import Mesh, PartitionSpec as P


B = 512
LANES = 128
SHARES = (1, 2, 2, 2, 1)
GROUPS = ((0,), (1, 2), (3, 4))
AHEAD = 2
OFFLOADED = (0,)
DEPTH = 4

CHIPS = ("z", "x", "y")
COLUMN = ("y", "k")
DEVICES = ("z", "x", "y", "k")
VMEM = pl.BlockSpec(memory_space=pltpu.VMEM)
SMEM = pl.BlockSpec(memory_space=pltpu.SMEM)
ANY = pl.BlockSpec(memory_space=pl.ANY)


def split(value):
    high = value.astype(jnp.bfloat16)
    low = (value - high.astype(jnp.float32)).astype(jnp.bfloat16)
    return high, low


def dot(left, right):
    return jnp.dot(left, right, preferred_element_type=jnp.float32)


def halve_kernel(tile_cols, tiles_ref, count_ref, inverse_ref, out_ref, held, made, sems, out_sems):
    count = count_ref[0]

    def fetch(step, slot):
        chosen = tiles_ref[step]
        row = pl.multiple_of(chosen // tile_cols * B, B)
        col = pl.multiple_of(chosen % tile_cols * B, B)
        return pltpu.make_async_copy(
            inverse_ref.at[pl.ds(row, B), pl.ds(col, B)], held.at[slot], sems.at[slot]
        )

    def put(step, slot):
        return pltpu.make_async_copy(made.at[slot], out_ref.at[step], out_sems.at[slot])

    for ahead in range(DEPTH - 1):

        @pl.when(ahead < count)
        def _():
            fetch(ahead, ahead).start()

    def step(index, carry):
        slot = lax.rem(index, DEPTH)
        side = lax.rem(index, 2)

        @pl.when(index + DEPTH - 1 < count)
        def _():
            fetch(index + DEPTH - 1, lax.rem(index + DEPTH - 1, DEPTH)).start()

        fetch(index, slot).wait()

        @pl.when(index >= 2)
        def _():
            put(index - 2, side).wait()

        high, low = split(held[slot])
        made[side, :, :B] = high
        made[side, :, B:] = low
        put(index, side).start()
        return carry

    lax.fori_loop(0, count, step, 0)
    for back in (2, 1):

        @pl.when(count >= back)
        def _():
            put(count - back, lax.rem(count - back, 2)).wait()


def halve(tiles, count, inverse):
    tile_rows, tile_cols = inverse.shape[0] // B, inverse.shape[1] // B
    return pl.pallas_call(
        functools.partial(halve_kernel, tile_cols),
        out_shape=jax.ShapeDtypeStruct((tile_rows * tile_cols, B, 2 * B), jnp.bfloat16),
        in_specs=[SMEM, SMEM, ANY],
        out_specs=ANY,
        scratch_shapes=[
            pltpu.VMEM((DEPTH, B, B), jnp.float32),
            pltpu.VMEM((2, B, 2 * B), jnp.bfloat16),
            pltpu.SemaphoreType.DMA((DEPTH,)),
            pltpu.SemaphoreType.DMA((2,)),
        ],
        cost_estimate=pl.CostEstimate(
            flops=0, bytes_accessed=8 * inverse.size, transcendentals=0
        ),
        name="halve",
    )(tiles, count, inverse)


def tiles_kernel(tile_cols, parts, tiles_ref, count_ref, place_ref, parts_ref, *refs):
    part_refs = refs[:parts]
    keep_ref, send_ref, highs, lows, total, held, came, sems, came_sems, out_sems = refs[parts:]
    count = count_ref[0]
    x, z, k = place_ref[0], place_ref[1], place_ref[2]
    cols, rows_each = part_refs[0].shape[0], part_refs[0].shape[1]

    def fetch(step, slot):
        return pltpu.make_async_copy(parts_ref.at[step], held.at[slot], sems.at[slot])

    for ahead in range(DEPTH - 1):

        @pl.when(ahead < count)
        def _():
            fetch(ahead, ahead).start()

    arrivals = [
        pltpu.make_async_copy(part_ref, came.at[index], came_sems.at[index])
        for index, part_ref in enumerate(part_refs)
    ]
    for arrival in arrivals:
        arrival.start()
    total[...] = jnp.zeros_like(total)
    for index in range(parts):
        half = lax.bitwise_xor(x, index) if parts == 2 else 0
        arrivals[index].wait()
        for j in range(cols):
            origin = lax.rem(z + j, cols)
            first = pl.multiple_of((half * cols + origin) * rows_each, rows_each)
            high, low = split(came[index, j])
            highs[pl.ds(first, rows_each), :] = high
            lows[pl.ds(first, rows_each), :] = low

    def step(index, carry):
        slot = lax.rem(index, DEPTH)

        @pl.when(index + DEPTH - 1 < count)
        def _():
            fetch(index + DEPTH - 1, lax.rem(index + DEPTH - 1, DEPTH)).start()

        fetch(index, slot).wait()
        chosen = tiles_ref[index]
        row = pl.multiple_of(chosen // tile_cols * B, B)
        col = pl.multiple_of(chosen % tile_cols * B, B)
        high, low = highs[pl.ds(col, B), :], lows[pl.ds(col, B), :]
        width = total.shape[1]
        if width == LANES:
            both = dot(held[slot, :, :B], jnp.concatenate([high, low], axis=1))
            product = both[:, :width] + both[:, width:] + dot(held[slot, :, B:], high)
        else:
            product = (
                dot(held[slot, :, :B], high)
                + dot(held[slot, :, B:], high)
                + dot(held[slot, :, :B], low)
            )
        total[pl.ds(row, B), :] += product
        return carry

    lax.fori_loop(0, count, step, 0)
    pairs, rows_out = keep_ref.shape[0], keep_ref.shape[1]
    copies = []
    for index, (out_ref, side) in enumerate(((send_ref, 1 - k), (keep_ref, k))):
        for pair in range(pairs):
            first = pl.multiple_of((2 * pair + side) * rows_out, rows_out)
            copies.append(
                pltpu.make_async_copy(
                    total.at[pl.ds(first, rows_out), :],
                    out_ref.at[pair],
                    out_sems.at[index * pairs + pair],
                )
            )
    for copy in copies:
        copy.start()
    for copy in copies:
        copy.wait()


def tile_products(tiles, count, place, halved, parts, rows, tile_cols):
    cols, _, width = parts[0].shape
    out = jax.ShapeDtypeStruct((cols // 2, rows // cols, width), jnp.float32)
    return pl.pallas_call(
        functools.partial(tiles_kernel, tile_cols, len(parts)),
        out_shape=(out, out),
        in_specs=[SMEM, SMEM, SMEM, ANY] + [ANY] * len(parts),
        out_specs=(ANY, ANY),
        scratch_shapes=[
            pltpu.VMEM((tile_cols * B, width), jnp.bfloat16),
            pltpu.VMEM((tile_cols * B, width), jnp.bfloat16),
            pltpu.VMEM((rows, width), jnp.float32),
            pltpu.VMEM((DEPTH, B, 2 * B), jnp.bfloat16),
            pltpu.VMEM((len(parts), *parts[0].shape), jnp.float32),
            pltpu.SemaphoreType.DMA((DEPTH,)),
            pltpu.SemaphoreType.DMA((len(parts),)),
            pltpu.SemaphoreType.DMA((cols,)),
        ],
        cost_estimate=pl.CostEstimate(
            flops=6 * rows * tile_cols * B * width,
            bytes_accessed=4 * rows * tile_cols * B,
            transcendentals=0,
        ),
        name="tiles",
    )(tiles, count, place, halved, *parts)


def turn_kernel(pairs, place_ref, *refs):
    out_ref = refs[-1]
    for index in range(pairs):
        value = refs[index][...] if pairs == 2 else refs[0][index]
        rows = value.shape[0]
        if pairs == 2:
            side = lax.bitwise_xor(place_ref[3], index)
            where = pl.ds(pl.multiple_of(side * rows, rows), rows)
        else:
            where = slice(index * rows, (index + 1) * rows)
        high, low = split(value.T)
        out_ref[0, :, where] = high
        out_ref[1, :, where] = low


def turn(place, factors, pairs, rows, width):
    return pl.pallas_call(
        functools.partial(turn_kernel, pairs),
        out_shape=jax.ShapeDtypeStruct((2, width, pairs * rows), jnp.bfloat16),
        in_specs=[SMEM] + [VMEM] * len(factors),
        out_specs=VMEM,
        name="turn",
    )(place, *factors)


def finish_kernel(swapped, place_ref, kept_ref, came_ref, turned_ref, sum_ref, term_ref):
    pairs, rows, width = kept_ref.shape
    for pair in range(pairs):
        sum_ref[pair] = kept_ref[pair] + came_ref[pair]
    high, low = split(sum_ref[...].reshape(pairs * rows, width))
    half = term_ref.shape[1]
    for index in range(2):
        side = lax.bitwise_xor(place_ref[2], index) if swapped else index
        left = pl.ds(pl.multiple_of(side * half, half), half)
        term_ref[index] = (
            dot(turned_ref[0, left, :], high)
            + dot(turned_ref[1, left, :], high)
            + dot(turned_ref[0, left, :], low)
        )


def finish(place, kept, came, turned, swapped):
    pairs, rows, step = kept.shape
    width = turned.shape[1]
    return pl.pallas_call(
        functools.partial(finish_kernel, swapped),
        out_shape=(
            jax.ShapeDtypeStruct(kept.shape, jnp.float32),
            jax.ShapeDtypeStruct((2, width // 2, step), jnp.float32),
        ),
        in_specs=[SMEM, VMEM, VMEM, VMEM],
        out_specs=(VMEM, VMEM),
        cost_estimate=pl.CostEstimate(
            flops=6 * pairs * rows * width * step,
            bytes_accessed=4 * pairs * rows * (width + 3 * step) + 4 * width * step,
            transcendentals=0,
        ),
        name="finish",
    )(place, kept, came, turned)


def stored_list(pattern, first_row, first_col, tile_rows, tile_cols):
    window = lax.dynamic_slice(pattern, (first_row, first_col), (tile_rows, tile_cols)).reshape(-1)
    count_all = tile_rows * tile_cols
    order = jnp.cumsum(window) - 1
    slots = jnp.arange(count_all, dtype=jnp.int32)
    chosen = (order[None, :] == slots[:, None]) & (window[None, :] > 0)
    return jnp.sum(jnp.where(chosen, slots[None, :], 0), axis=1), jnp.sum(window)[None]


def swap(value, axis):
    return lax.ppermute(value, axis, [(0, 1), (1, 0)])


def sum_scatter(value, axes):
    return jnp.sum(lax.all_to_all(value, axes, split_axis=0, concat_axis=0), axis=0)


def spread(value, axes):
    copies = jnp.broadcast_to(value[None], (lax.axis_size(axes), *value.shape))
    return lax.all_to_all(copies, axes, split_axis=0, concat_axis=0)


def pick(pair, index):
    return lax.dynamic_index_in_dim(pair, index, 0, False)


def routes(planes, cols, turn_index):
    ratio = 2 * planes // cols
    pairs = []
    for z in range(planes):
        for x in range(2):
            for col in range(cols):
                if ratio == 1 and col % 2 != x:
                    continue
                source = ((col * ratio // 2) * 2 + x) * cols + (z + turn_index) % cols
                pairs.append((source, (z * 2 + x) * cols + col))
    return pairs


def shares(width):
    return SHARES if sum(SHARES) * LANES == width else (1,) * (width // LANES)


def after(value, others):
    return lax.optimization_barrier((value, others))[0]


def step_body(inverse, pattern, factor, diag_inverse):
    planes, cols = lax.axis_size("z"), lax.axis_size(COLUMN)
    x, y, z, k = (lax.axis_index(a) for a in ("x", "y", "z", "k"))
    column = lax.axis_index(COLUMN)
    ratio = 2 * planes // cols
    rows_each, width = factor.shape
    tile_rows, tile_cols = inverse.shape[0] // B, inverse.shape[1] // B
    tiles, count = stored_list(
        pattern, (z * 2 + x) * tile_rows, column * tile_cols, tile_rows, tile_cols
    )
    place = jnp.stack([x, z, k, y]).astype(jnp.int32)
    chips = lax.axis_size(CHIPS)
    pairs = cols // 2
    if pairs == 2:
        factors = (factor, swap(factor, "y"))
    else:
        factors = (lax.all_gather(factor, "y", axis=0),)
    halved = halve(tiles, count, inverse)
    turned = turn(place, factors, pairs, rows_each, width)
    arrivals, panels, terms = [], [], []
    pieces, spreads, pending, diags = {}, {}, {}, {}
    first = 0
    groups = groups_of(len(shares(width)))
    for chunk, share in enumerate(shares(width)):
        step = share * LANES
        part = factor[:, first : first + step]
        first += step
        if chunk >= AHEAD:
            part = after(part, arrivals[chunk - AHEAD])
        mine = []
        for j in range(cols):
            mine.append(lax.ppermute(part, DEVICES, routes(planes, cols, j)))
        arrivals.append(mine)
        mine = jnp.stack(mine)
        theirs = swap(mine, "x")
        parts = (mine, theirs) if ratio == 2 else (jnp.where(column % 2 == x, mine, theirs),)
        gate = after(place, pieces[chunk - 2]) if chunk - 2 in pieces else place
        kept, send = tile_products(
            tiles, count, gate, halved, parts, inverse.shape[0], tile_cols
        )
        for index, (born, state, value) in list(pending.items()):
            value = after(value, kept)
            if state == 0:
                piece = jnp.sum(value, axis=0)
                pieces[chunk - 1] = piece
                pending[index] = (born, 1, spread(piece, CHIPS))
            else:
                spreads[born] = value
                del pending[index]
                diags[index] = assemble(value, width, k)
        came = swap(send, "k")
        gate = after(place, spreads[chunk - 2]) if chunk - 2 in spreads else place
        summed, term = finish(gate, kept, came, turned, chunk not in groups[0])
        terms.append(term)
        if pairs == 2:
            panels.append(-(pick(summed, y) + swap(pick(summed, 1 - y), "y")))
        else:
            panels.append(-sum_scatter(summed, "y"))
        for index, group in enumerate(groups):
            if not group or group[-1] != chunk:
                continue
            mine = [terms[member] for member in group]
            if index in OFFLOADED:
                diags[index] = lax.psum([term.reshape(width, -1) for term in mine], DEVICES)
                continue
            half = jnp.concatenate([term[0] for term in mine], 1) + swap(
                jnp.concatenate([term[1] for term in mine], 1), "k"
            )
            sent = half.reshape(chips, -1, half.shape[1])
            value = lax.all_to_all(sent, CHIPS, split_axis=0, concat_axis=0)
            pending[index] = (chunk, 0, value)
    for index, (_, state, value) in sorted(pending.items()):
        if state == 0:
            value = spread(jnp.sum(value, axis=0), CHIPS)
        diags[index] = assemble(value, width, k)
    starts = [sum(shares(width)[:chunk]) * LANES for chunk in range(len(panels) + 1)]
    total = diag_inverse
    for index in sorted(diags, key=lambda index: 1.5 if index in OFFLOADED else index):
        pieces = diags[index]
        members = groups[index]
        for piece, chunk in zip(pieces, members if index in OFFLOADED else members[:1]):
            first = starts[chunk]
            columns = total[:, first : first + piece.shape[1]] + piece
            total = lax.dynamic_update_slice(total, columns, (0, first))
    return jnp.concatenate(panels, 1), total


def assemble(value, width, k):
    full = value.reshape(width // 2, -1)
    far = swap(full, "k")
    return [jnp.concatenate([jnp.where(k == 0, full, far), jnp.where(k == 0, far, full)], 0)]


def groups_of(chunks):
    return GROUPS if chunks == len(SHARES) else ((), tuple(range(chunks)))


def solution(mesh):
    rows, cols = mesh.shape["row"], mesh.shape["col"]
    grid = Mesh(mesh.devices.reshape(rows // 2, 2, cols // 2, 2), DEVICES)
    return jax.shard_map(
        step_body,
        mesh=grid,
        in_specs=(P(("z", "x"), ("y", "k")), P(), P(DEVICES, None), P()),
        out_specs=(P(DEVICES, None), P()),
        check_vma=False,
    )
```
